32 devices in a mesh: dp: 16 (over z, y, core), mp: 2 (over x).
Axes of the slice: x: 2, y: 2, z: 4, core: 2. Of those that a mesh axis runs over, the one named last changes fastest.
Arguments:
- inputs: bfloat16 [4096, 2048], P('dp', 'mp'), may hold values from -11 to 11
- next_inputs: bfloat16 [4096, 2048], P('dp', 'mp'), may hold values from -6 to 6
- cotangent: bfloat16 [4096, 1792], P('dp', 'mp'), may hold values from -11 to 11
- master: float32 [2048, 1792], P('dp', 'mp'), may hold values from -0.125 to 0.125
- first_moment: float32 [2048, 1792], P('dp', 'mp'), may hold values from -18 to 18
- second_moment: float32 [2048, 1792], P('dp', 'mp'), may hold values from 1 to 100
Outputs:
- input_grad: bfloat16 [4096, 2048], P('dp')
- next_up: bfloat16 [4096, 1792], P('dp', 'mp')
- new_master: float32 [2048, 1792], P('dp', 'mp')
- new_first: float32 [2048, 1792], P('dp', 'mp')
- new_second: float32 [2048, 1792], P('dp', 'mp')
The draws below stay inside these ranges and needn't reach their ends.
All inputs are finite; a program needn't handle non-finite values.
Results may differ from the reference program's by a relative error of at most 0.004.
The reference program's roundings to bfloat16 on the way (of `weights` and `new_weights`) count: a program that leaves them out, or rounds other values in their place, can miss the bound.
Values may be sent and summed in bfloat16 or wider, within the bound.
No kernel may reach another device: no remote copies, remote signals or barrier semaphores. Data moves between devices by JAX's collectives and lax.ppermute only.
A program may use at most 64 MiB of HBM per device.

```python
import math
import jax
import jax.numpy as jnp
from jax import lax

D = 2048
TOK_DEV = 256
FF = 1792
TOKENS = 4096
N_DP = 16


def signed_magnitudes(key, count, low):
    sign_key, size_key = jax.random.split(key)
    signs = jnp.where(jax.random.bernoulli(sign_key, 0.5, (count,)), 1.0, -1.0).astype(jnp.float32)
    sizes = jax.random.uniform(size_key, (count,), jnp.float32, low, 1.0)
    return signs * sizes


def shared_factors(key):
    base = jax.random.fold_in(key, 7001)
    feat_key = jax.random.fold_in(base, 1)
    unit_key = jax.random.fold_in(base, 2)
    block_key = jax.random.fold_in(base, 3)
    feature_dir = signed_magnitudes(feat_key, D, 0.8)
    hidden_dir = signed_magnitudes(unit_key, FF, 0.8)
    blocks = TOKENS // TOK_DEV
    half_weights = signed_magnitudes(block_key, blocks // 2, 0.7)
    block_weights = jnp.concatenate([half_weights, -half_weights])
    token_weights = jnp.repeat(block_weights, TOK_DEV, total_repeat_length=TOKENS)
    return (feature_dir, hidden_dir, token_weights)


def noise_field(key, shape):
    return jnp.clip(jax.random.normal(key, shape, jnp.float32), -4.0, 4.0)


def strength():
    return 6.0


def draw_inputs(key, part):
    feature_dir, hidden_dir, token_weights = shared_factors(key)
    noise = noise_field(jax.random.fold_in(key, 11), (TOKENS, D))
    values = noise + strength() * feature_dir[None, :]
    return values.astype(jnp.bfloat16)


def draw_cotangent(key, part):
    feature_dir, hidden_dir, token_weights = shared_factors(key)
    noise = noise_field(jax.random.fold_in(key, 23), (TOKENS, FF))
    values = noise + strength() * token_weights[:, None] * hidden_dir[None, :]
    return values.astype(jnp.bfloat16)


def spiked(result, rng, source, target, parts, factor):
    owner, partner = [(jnp.arange(result.shape[axis_at]) // (result.shape[axis_at] // parts)).reshape([-1 if axis == axis_at else 1 for axis in range(result.ndim)]) for axis_at in (source, target)]
    chosen = jax.random.permutation(rng, parts)[partner]
    strong = (owner == chosen) | (owner == (partner + parts // 2) % parts)
    return jnp.where(strong, factor * result, result)


def steps_of(rng, shape, shards, smallest, top_value):
    def one(dim, blocks):
        draws = jax.random.uniform(jax.random.fold_in(jax.random.fold_in(rng, 6), dim), (blocks,), jnp.float32, smallest / len(shards), top_value / len(shards))
        return jnp.repeat(jnp.exp(draws), shape[dim] // blocks).reshape((-1,) + (1,) * (len(shape) - dim - 1))

    gain = one(*shards[0])
    for cut in shards[1:]:
        gain = gain * one(*cut)
    return gain


def centred(rng, dims, width, limit, cuts=(), held_as=jnp.bfloat16):
    values = width * jax.random.normal(rng, dims, jnp.float32)
    if cuts:
        values = values * steps_of(rng, dims, cuts, -0.22, 0.18)
    return jnp.clip(values, -limit, limit).astype(held_as)


def gaussian_with(own_key, shape, deviation, limit, pieces, heavy, held_as=jnp.bfloat16):
    values = deviation * jax.random.normal(own_key, shape, jnp.float32)
    if pieces:
        values = values * steps_of(own_key, shape, pieces, -0.22, 0.18)
    return jnp.clip(spiked(values, jax.random.fold_in(own_key, 3), *heavy), -limit, limit).astype(held_as)


def setup_inputs(seed: int = 0) -> dict:
    key_list = jax.random.split(jax.random.key(seed), 7)
    return {
        "inputs": draw_inputs(jax.random.fold_in(key_list[6], 71), 0),
        "next_inputs": gaussian_with(key_list[1], (TOKENS, D), 1.0, 6.0, ((0, 16), (1, 2)), (0, 1, 16, 2.0)),
        "cotangent": draw_cotangent(jax.random.fold_in(key_list[6], 71), 0),
        "master": centred(key_list[3], (D, FF), D ** -0.5, 0.125, ((0, 16), (1, 2)), jnp.float32),
        "first_moment": centred(key_list[4], (D, FF), 3.0, 18.0, ((0, 16), (1, 2)), jnp.float32),
        "second_moment": jnp.clip(jnp.exp(math.log(100.0) - 4.6051702 * jax.random.uniform(key_list[5], (D, FF), jnp.float32) ** steps_of(key_list[5], (D, FF), ((0, 16), (1, 2)), -0.2, 0.2)), 1.0, 100.0),
    }


def reference(inputs, next_inputs, cotangent, master, first_moment, second_moment):
    weights = master.astype(jnp.bfloat16)
    input_grad = jnp.dot(cotangent, weights.T, preferred_element_type=jnp.float32).astype(jnp.bfloat16)

    def add_block(index, total):
        start = (jnp.asarray(index) * TOK_DEV).astype(jnp.int32)
        rows_in = lax.dynamic_slice_in_dim(inputs, start, TOK_DEV, 0)
        rows_out = lax.dynamic_slice_in_dim(cotangent, start, TOK_DEV, 0)
        term = jnp.dot(rows_in.T, rows_out, preferred_element_type=jnp.float32)
        return total + term
    grad = lax.fori_loop(0, N_DP, add_block, jnp.zeros((D, FF), jnp.float32))
    new_first = 0.9 * first_moment + 0.1 * grad
    new_second = 0.95 * second_moment + 0.05 * grad * grad
    update = new_first / (1.0 - 0.9 ** 10) / (jnp.sqrt(new_second / (1.0 - 0.95 ** 10)) + 1e-08)
    new_master = master - 0.003 * (update + 0.1 * master)
    new_weights = new_master.astype(jnp.bfloat16)
    next_up = jnp.dot(next_inputs, new_weights, preferred_element_type=jnp.float32).astype(jnp.bfloat16)
    return (input_grad, next_up, new_master, new_first, new_second)
```

```python
import jax
import jax.numpy as jnp
from jax import lax
from jax.sharding import PartitionSpec as P


def picked(index, choices):
    value = choices[0]
    for at, choice in enumerate(choices[1:], 1):
        value = jnp.where(index == at, choice, value)
    return value


def split_by(bit, left, right):
    return jnp.where(bit, right, left), jnp.where(bit, left, right)


def build(n_dp, n_mp):
    n_hi, n_lo = n_mp, n_dp // n_mp
    lo_bits = []
    bit = n_lo // 2
    while bit:
        lo_bits.append(bit)
        bit //= 2
    dp_bits = []
    bit = n_dp // 2
    while bit:
        dp_bits.append(bit)
        bit //= 2

    def over_dp(value, offset):
        return lax.ppermute(value, "dp", [(d, d ^ offset) for d in range(n_dp)])

    def over_mp(value, offset):
        return lax.ppermute(value, "mp", [(m, m ^ offset) for m in range(n_mp)])

    def gathered(block, bits):
        held = [(0, block)]
        for bit in bits:
            held = held + [(offset ^ bit, over_dp(value, bit)) for offset, value in held]
        return held

    def shards(inputs, next_inputs, cotangent, master, first_moment, second_moment):
        tokens = inputs.shape[0]
        d, m = lax.axis_index("dp"), lax.axis_index("mp")
        hi = d // n_lo

        piece = inputs
        for bit in lo_bits:
            half = piece.shape[1] // 2
            keep, send = split_by((d & bit) != 0, piece[:, :half], piece[:, half:])
            piece = jnp.concatenate([keep, over_dp(send, bit)], axis=0)
        pieces = [piece] + [over_mp(piece, j) for j in range(1, n_mp)]

        cotangents = jnp.concatenate([value for _, value in gathered(cotangent, lo_bits)], axis=0)

        def gradient_of(block):
            rows = picked(m ^ block, pieces)
            return lax.dot_general(
                rows, cotangents, (((0,), (0,)), ((), ())), preferred_element_type=jnp.float32
            )

        received = [over_dp(gradient_of(hi ^ j), j * n_lo) for j in range(1, n_hi)]
        grad = gradient_of(hi)
        for value in received:
            grad = grad + value

        new_first = 0.9 * first_moment + 0.1 * grad
        new_second = 0.95 * second_moment + 0.05 * grad * grad
        update = new_first / (1.0 - 0.9**10) / (jnp.sqrt(new_second / (1.0 - 0.95**10)) + 1e-08)
        new_master = master - 0.003 * (update + 0.1 * master)

        weights = master.astype(jnp.bfloat16)
        blocks = [weights] + [over_dp(weights, j * n_lo) for j in range(1, n_hi)]

        def contribution_to(block):
            rows = picked(hi ^ block, blocks)
            return lax.dot_general(
                cotangents, rows, (((1,), (1,)), ((), ())), preferred_element_type=jnp.float32
            )

        shares = [over_mp(contribution_to(m ^ j), j) for j in range(1, n_mp)]
        summed = contribution_to(m)
        for value in shares:
            summed = summed + value
        back = summed.astype(jnp.bfloat16)
        for bit in reversed(lo_bits):
            half = back.shape[0] // 2
            other = over_dp(back[half:], bit)
            back = jnp.where(
                (d & bit) != 0,
                jnp.concatenate([other, back[:half]], axis=1),
                jnp.concatenate([back[:half], other], axis=1),
            )
        halves = [back] + [over_mp(back, j) for j in range(1, n_mp)]
        input_grad = jnp.concatenate([picked(m ^ at, halves) for at in range(n_mp)], axis=1)

        near = [next_inputs] + [over_mp(next_inputs, j) for j in range(1, n_mp)]
        features = jnp.concatenate([picked(m ^ at, near) for at in range(n_mp)], axis=1)
        for bit in dp_bits:
            width = features.shape[1] // n_dp * bit
            parts = features.reshape(tokens, -1, 2, width)
            features = jnp.where(
                (d & bit) != 0, jnp.concatenate([parts[:, :, 1:], parts[:, :, :1]], axis=2), parts
            ).reshape(tokens, -1)
        width = features.shape[1] // n_dp
        held = gathered(new_master.astype(jnp.bfloat16), dp_bits)
        ordered = jnp.concatenate(
            [features[:, offset * width : (offset + 1) * width] for offset, _ in held], axis=1
        )
        new_weights = jnp.concatenate([value for _, value in held], axis=0)
        next_up = jnp.dot(ordered, new_weights, preferred_element_type=jnp.float32)
        return (input_grad, next_up.astype(jnp.bfloat16), new_master, new_first, new_second)

    return shards


def solution(mesh):
    placed = P("dp", "mp")
    return jax.shard_map(
        build(mesh.shape["dp"], mesh.shape["mp"]),
        mesh=mesh,
        in_specs=(placed,) * 6,
        out_specs=(P("dp", None), placed, placed, placed, placed),
        check_vma=False,
    )
```
